256 devices in a mesh: blk: 32 (over z, x_lo, core), fiber: 8 (over y, x_hi).
Axes of the slice: x: 4 (x_hi: 2, x_lo: 2; x = x_hi * 2 + x_lo), y: 4, z: 8, core: 2. Of those that a mesh axis runs over, the one named last changes fastest.
Arguments:
- queries: bfloat16 [65536, 256], P(('blk', 'fiber')), may hold values from -6 to 6
- keys: bfloat16 [65536, 256], P(('blk', 'fiber')), may hold values from -6 to 6
- values: bfloat16 [65536, 256], P(('blk', 'fiber')), may hold values from -6 to 6
- tiles: int32 [32, 8, 4, 16], P('blk', 'fiber'), may hold values from -1 to 31, as said below
- edges: bfloat16 [32, 8, 4, 16, 128, 128], P('blk', 'fiber'), may hold values from 0.05 to 2, as said below
Outputs:
- attended: bfloat16 [65536, 256], P(('blk', 'fiber'))
The draws below stay inside these ranges and needn't reach their ends.
Inputs may be any that keep to these rules, and one draw needn't show every extreme that they name: tiles[b, f, s, :] lists the occupied tiles between query block b and key subblock f of block (b - s) mod 32: distinct numbers r * 2 + c (row tile r, column tile c) in the first slots, then -1 in the slots left over. Each list holds at least one tile, and in every draw some list is full. edges[c, f, s, k] holds the edge values of the tile in slot k of the list tiles[(c + s) mod 32, f, s]; slots marked -1 there hold values of no edge.
All inputs are finite; a program needn't handle non-finite values.
Results may differ from the reference program's by a relative error of at most 0.0049.
Values may be sent and summed in bfloat16 or wider, within the bound.
A program may use at most 128 MiB of HBM per device.

```python
import jax
import jax.numpy as jnp
from jax import lax

F = 256
HEADS = 4
TILE = 128
KS = 256
STOPS = 4
DH = 64
BLOCKS = 32
FIBERS = 8
ROWS = 2048
NODES = 65536
TILES_PAIR = 32
CAP = 16
N_FIBER = 8


def draw_tiles(key, part):
    list_count = BLOCKS * FIBERS * STOPS
    list_keys = jax.random.split(jax.random.fold_in(key, 11), list_count)
    shuffled = jax.vmap(lambda single: jax.random.permutation(single, TILES_PAIR))(list_keys)[:, :CAP]
    counts = jax.random.randint(jax.random.fold_in(key, 12), (list_count,), 1, CAP + 1)
    chosen = jax.random.randint(jax.random.fold_in(key, 13), (), 0, list_count)
    counts = jnp.where(jnp.arange(list_count) == chosen, CAP, counts)
    slot_ids = jnp.where(jnp.arange(CAP)[None, :] < counts[:, None], shuffled, -1)
    return slot_ids.reshape(BLOCKS, FIBERS, STOPS, CAP).astype(jnp.int32)


def draw_edges(key, part):
    shape = (BLOCKS, FIBERS, STOPS, CAP, TILE, TILE)
    drawn = jax.random.uniform(jax.random.fold_in(key, 23), shape, jnp.float32, 0.1, 1.5)
    return drawn.astype(jnp.bfloat16)


def levels(rng, shape, shards, low, high):
    gain, own = 1.0, jax.random.fold_in(rng, 6)
    for axis_at, shards_of in shards:
        heights = jnp.exp(jax.random.uniform(jax.random.fold_in(own, axis_at), (shards_of,), jnp.float32, low / len(shards), high / len(shards)))
        gain = gain * jnp.repeat(heights, shape[axis_at] // shards_of).reshape([-1 if axis == axis_at else 1 for axis in range(len(shape))])
    return gain


def normal_values(stream_key, extent, scale, reach, cuts=(), kind=jnp.bfloat16):
    values = scale * jax.random.normal(stream_key, extent, jnp.float32)
    if cuts:
        values = values * levels(stream_key, extent, cuts, -0.22, 0.18)
    return jnp.clip(values, -reach, reach).astype(kind)


def setup_inputs(seed: int = 0) -> dict:
    arg_keys = jax.random.split(jax.random.key(seed), 6)
    queries = normal_values(arg_keys[0], (NODES, F), 1.0, 6.0, ((0, 256),))
    keys = normal_values(arg_keys[1], (NODES, F), 1.0, 6.0, ((0, 256),))
    values = normal_values(arg_keys[2], (NODES, F), 1.0, 6.0, ((0, 256),))
    tiles = draw_tiles(jax.random.fold_in(arg_keys[5], 71), 0)
    edges = draw_edges(jax.random.fold_in(arg_keys[5], 71), 0)
    return {"queries": queries, "keys": keys, "values": values, "tiles": tiles, "edges": edges}


LEAKY_SLOPE = 0.2

def reference(queries, keys, values, tiles, edges):
    row_tiles = ROWS // TILE
    key_tiles = KS // TILE
    score_scale = DH ** (-0.5)
    edge_scale = (STOPS * N_FIBER * KS / 4) ** (-0.5)
    highest = lax.Precision.HIGHEST
    query_blocks = queries.reshape(BLOCKS, row_tiles, TILE, F)
    key_blocks = keys.reshape(BLOCKS, FIBERS, key_tiles, TILE, F)
    value_blocks = values.reshape(BLOCKS, FIBERS, key_tiles, TILE, F)

    def per_block(block_index):
        query_tiles = query_blocks[block_index]

        def one_list(running, combo_index):
            numerator, denominator = running
            fiber_index = combo_index // STOPS
            stop_index = combo_index % STOPS
            owner_block = (block_index - stop_index + BLOCKS) % BLOCKS
            slot_ids = tiles[block_index, fiber_index, stop_index]
            in_use = slot_ids >= 0
            safe_ids = jnp.where(in_use, slot_ids, 0).astype(jnp.int32)
            row_tile = (safe_ids // key_tiles).astype(jnp.int32)
            col_tile = (safe_ids % key_tiles).astype(jnp.int32)
            query_sel = query_tiles[row_tile].astype(jnp.float32).reshape(CAP, TILE, HEADS, DH)
            key_sel = key_blocks[owner_block, fiber_index][col_tile].astype(jnp.float32).reshape(CAP, TILE, HEADS, DH)
            value_sel = value_blocks[owner_block, fiber_index][col_tile].astype(jnp.float32).reshape(CAP, TILE, HEADS, DH)
            scores = jnp.einsum('gqhd,gkhd->ghqk', query_sel, key_sel, precision=highest) * score_scale
            slot_edges = edges[owner_block, fiber_index, stop_index].astype(jnp.float32)
            weights = jnp.where(scores > 0, scores, LEAKY_SLOPE * scores) * slot_edges[:, None] * edge_scale
            weights = weights * in_use[:, None, None, None].astype(jnp.float32)
            squares = lax.optimization_barrier(jnp.sum(weights * weights, axis=3))
            denominator = denominator + jax.ops.segment_sum(squares, row_tile, num_segments=row_tiles)
            rounded = lax.optimization_barrier(weights.astype(jnp.bfloat16)).astype(jnp.float32)
            blended = jnp.einsum('ghqk,gkhd->gqhd', rounded, value_sel, precision=highest).reshape(CAP, TILE, F)
            numerator = numerator + jax.ops.segment_sum(blended, row_tile, num_segments=row_tiles)
            return ((numerator, denominator), None)
        start_pair = (jnp.zeros((row_tiles, TILE, F), jnp.float32), jnp.zeros((row_tiles, HEADS, TILE), jnp.float32))
        (numerator, denominator), _ = lax.scan(one_list, start_pair, jnp.arange(FIBERS * STOPS, dtype=jnp.int32))
        spread = jnp.sqrt(1.0 + jnp.transpose(denominator, (0, 2, 1)))
        result = numerator.reshape(row_tiles, TILE, HEADS, DH) / spread[..., None]
        return result.reshape(ROWS, F).astype(jnp.bfloat16)
    blocks_out = lax.map(per_block, jnp.arange(BLOCKS, dtype=jnp.int32))
    return blocks_out.reshape(NODES, F)
```

```python
import functools

import jax
import jax.numpy as jnp
from jax import lax
from jax.experimental import pallas as pl
from jax.experimental.pallas import tpu as pltpu
from jax.sharding import PartitionSpec as P

HEADS = 4
LEAKY_SLOPE = 0.2
MESH = pl.DeviceIdType.MESH
HIGHEST = lax.Precision.HIGHEST

ORDER = [(2, 1), (2, 0), (1, 1), (1, 0), (3, 1), (3, 0), (0, 1), (0, 0)]
PLACE = {d: j for j, d in enumerate(ORDER)}


def kernel(
    tiles, q_hbm, k_hbm, v_hbm, e_hbm, out,
    q_all, kv, e0, e1, e2, e3, er1, er2, kvr, inv_v, inv_s,
    kmask, vmask, edense, numacc, denacc, sendbuf, dsend, nrecv, drecv,
    local_sem, q_send, q_recv, e_send, e_recv, kv_send, kv_recv, kvf_send,
    relay_send, relay_recv, inv_sem, n_send, n_recv, d_send, d_recv,
):
    blocks = lax.axis_size("blk")
    b = lax.axis_index("blk")
    f = lax.axis_index("fiber")
    place = b % 4
    y = f // 2
    xh = f % 2
    even = place % 2 == 0
    stops, cap, tile, _ = e_hbm.shape
    rows, feat = q_hbm.shape
    dh = feat // HEADS
    scale = float(dh ** -0.5 * (stops * 8 * rows / 4) ** -0.5)
    ebufs = (e0, e1, e2, e3)

    def at(db, flip=False):
        fb = 1 - xh if flip else xh
        return ((b + db + blocks) % blocks, y * 2 + fb)

    def fiber_at(dy, dx):
        return ((y + dy) % 4) * 2 + (xh + dx) % 2

    def place_at(j):
        k = j // 2
        dy = jnp.where(k == 0, 2, jnp.where(k == 1, 1, jnp.where(k == 2, 3, 0)))
        return fiber_at(dy, 1 - j % 2)

    def remote(src, dst, ssem, rsem, dev):
        return pltpu.make_async_remote_copy(
            src_ref=src, dst_ref=dst, send_sem=ssem, recv_sem=rsem,
            device_id=dev, device_id_type=MESH,
        )

    locals_ = [
        pltpu.make_async_copy(q_hbm, q_all.at[f], local_sem.at[0]),
        pltpu.make_async_copy(k_hbm, kv.at[0, 0], local_sem.at[1]),
        pltpu.make_async_copy(v_hbm, kv.at[0, 1], local_sem.at[2]),
        pltpu.make_async_copy(e_hbm.at[0], e0, local_sem.at[3]),
    ]
    for c in locals_:
        c.start()

    lane = lax.broadcasted_iota(jnp.int32, (8, 128), 1)
    row = lax.broadcasted_iota(jnp.int32, (8, 128), 0)
    slots = jnp.full((8, 128), -1, jnp.int32)
    for s in range(stops):
        for k in range(cap):
            slots = jnp.where((lane == tiles[s, k]) & (row == s), k, slots)
    inv_v[0] = slots

    barrier = pltpu.get_barrier_semaphore()
    partners = [at(d) for d in (-4, -3, -2, -1, 1, 2, 3, 4)]
    partners += [at(d, True) for d in (-2, -1, 1, 2)]
    partners += [(b, fiber_at(dy, dx)) for dy, dx in ORDER[:-1]]
    for dev in partners:
        pl.semaphore_signal(barrier, 1, device_id=dev, device_id_type=MESH)
    pl.semaphore_wait(barrier, len(partners))

    own_q = [
        remote(q_hbm, q_all.at[f], q_send.at[PLACE[d]], q_recv.at[PLACE[d]], (b, fiber_at(-d[0], d[1])))
        for d in ((0, 1), (3, 0), (1, 0), (2, 0))
    ]
    for c in own_q:
        c.start()
    inv_copy = remote(inv_v.at[0], inv_v.at[1], inv_sem.at[0], inv_sem.at[1], (b, fiber_at(0, 1)))
    inv_copy.start()

    def send_e(s, slot, dev):
        return remote(e_hbm.at[s], ebufs[slot], e_send.at[s], e_recv.at[slot], dev)

    def send_kv(n, slot, dev):
        return [
            remote(k_hbm, kv.at[slot, 0], kv_send.at[n, 0], kv_recv.at[slot, 0], dev),
            remote(v_hbm, kv.at[slot, 1], kv_send.at[n, 1], kv_recv.at[slot, 1], dev),
        ]

    sends = {
        0: send_kv(0, 2, at(2)) + [send_e(2, 2, at(2)), send_e(3, 3, at(3))]
        + send_kv(1, 1, at(1)) + [send_e(1, 1, at(1))],
        1: send_kv(0, 1, at(1, True)) + send_kv(1, 1, at(3))
        + [send_e(1, 1, at(1, True)), send_e(3, 1, at(3)), send_e(2, 2, at(2, True))],
        2: send_kv(0, 2, at(2)) + [send_e(2, 2, at(2)), send_e(3, 2, at(3))]
        + send_kv(1, 1, at(1)) + [send_e(1, 1, at(1))],
        3: [
            remote(k_hbm, kvr.at[0], kv_send.at[0, 0], relay_recv.at[2], at(-2, True)),
            remote(v_hbm, kvr.at[1], kv_send.at[0, 1], relay_recv.at[3], at(-2, True)),
            remote(e_hbm.at[1], er1, e_send.at[1], relay_recv.at[0], at(-2, True)),
            remote(e_hbm.at[2], er2, e_send.at[2], relay_recv.at[1], at(-2, True)),
        ]
        + send_kv(1, 3, at(3)) + [send_e(3, 3, at(3))],
    }
    for p in range(4):
        @pl.when(place == p)
        def _():
            for c in sends[p]:
                c.start()

    pf = fiber_at(0, 1)
    remote(q_hbm, q_all.at[pf], q_send.at[6], q_recv.at[6], (b, pf)).wait_recv()
    other_q = [
        remote(q_all.at[pf], q_all.at[pf], q_send.at[PLACE[d]], q_recv.at[PLACE[d]], (b, fiber_at(-d[0], 0)))
        for d in ((3, 1), (1, 1), (2, 1))
    ]
    for c in other_q:
        c.start()

    inv_copy.wait_recv()
    inv_local = pltpu.make_async_copy(inv_v, inv_s, local_sem.at[4])
    inv_local.start()

    relays = [
        remote(kvr.at[0], kv.at[3, 0], relay_send.at[2], kv_recv.at[3, 0], at(3)),
        remote(kvr.at[1], kv.at[3, 1], relay_send.at[3], kv_recv.at[3, 1], at(3)),
        remote(er1, e3, relay_send.at[0], e_recv.at[3], at(3)),
        remote(er2, e3, relay_send.at[1], e_recv.at[3], at(4)),
    ]
    relay_in = [
        remote(k_hbm, kvr.at[0], kv_send.at[0, 0], relay_recv.at[2], at(3)),
        remote(v_hbm, kvr.at[1], kv_send.at[0, 1], relay_recv.at[3], at(3)),
        remote(e_hbm.at[1], er1, e_send.at[1], relay_recv.at[0], at(3)),
        remote(e_hbm.at[2], er2, e_send.at[2], relay_recv.at[1], at(3)),
    ]

    @pl.when(place == 1)
    def _():
        for i in (0, 1, 2):
            relay_in[i].wait_recv()
            relays[i].start()

    for c in locals_:
        c.wait()
    inv_local.wait()

    stop_of = [
        jnp.int32(0),
        jnp.where(place == 0, 3, 1),
        jnp.where(place == 1, 3, 2),
        jnp.where(place == 0, 1, jnp.where(place == 1, 2, 3)),
    ]
    from_partner = [
        jnp.int32(0),
        jnp.where(place == 2, 1, 0),
        jnp.where(place == 3, 1, 0),
        jnp.where(place <= 1, 1, 0),
    ]

    lane_half = lax.broadcasted_iota(jnp.int32, (rows, 2 * dh), 1) // dh

    def split_heads(slot):
        for h in range(HEADS):
            cols = pl.ds((h // 2) * 2 * dh, 2 * dh)
            keep = lane_half == h % 2
            kmask[h] = jnp.where(keep, kv[slot, 0, :, cols], jnp.zeros((), jnp.bfloat16))
            vmask[h] = jnp.where(keep, kv[slot, 1, :, cols], jnp.zeros((), jnp.bfloat16))

    def chunk(slot, fc):
        ebuf = ebufs[slot]
        for rr in range(rows // tile):
            for c in range(rows // tile):
                n = fc * 4 + (rr * 2 + c)
                code = inv_s[from_partner[slot], stop_of[slot], n]
                weight = jnp.where(code >= 0, scale, 0.0).astype(jnp.float32)
                edense[pl.ds(rr * tile, tile), pl.ds(c * tile, tile)] = (
                    ebuf[jnp.maximum(code, 0)].astype(jnp.float32) * weight
                )
        for pair in range(HEADS // 2):
            cols = pl.ds(pair * 2 * dh, 2 * dh)
            q = q_all[fc, :, cols]
            part = None
            for hh in range(2):
                h = pair * 2 + hh
                score = lax.dot_general(
                    q, kmask[h], (((1,), (1,)), ((), ())), preferred_element_type=jnp.float32
                )
                w = jnp.maximum(score, LEAKY_SLOPE * score) * edense[...]
                sq = w * w
                sq = sq[:, :tile] + sq[:, tile:]
                blend = jnp.dot(w.astype(jnp.bfloat16), vmask[h], preferred_element_type=jnp.float32)
                part = blend if part is None else part + blend
                if slot == 0:
                    denacc[h, fc] = sq
                else:
                    denacc[h, fc] += sq
            if slot == 0:
                numacc[fc, :, cols] = part
            else:
                numacc[fc, :, cols] += part

    split_heads(0)

    @pl.loop(0, 8)
    def _(i):
        j = 7 - i

        @pl.when((j < 6))
        def _():
            fc = place_at(j)
            remote(q_hbm, q_all.at[fc], q_send.at[j], q_recv.at[j], (b, pf)).wait_recv()

        chunk(0, place_at(j))

    @pl.when(place == 1)
    def _():
        relay_in[3].wait_recv()
        relays[3].start()

    def kv_wait(slot):
        for c in send_kv(0, slot, at(1)):
            c.wait_recv()

    def kv_forward(n, slot, to):
        return [
            remote(kv.at[slot, i], kv.at[to, i], kvf_send.at[n, i], kv_recv.at[to, i], at(1))
            for i in range(2)
        ]

    forwards = {
        1: {2: kv_forward(0, 1, 2)},
        2: {0: kv_forward(0, 2, 2), 2: kv_forward(1, 2, 3)},
        3: {0: kv_forward(1, 3, 3)},
    }
    for slot in range(1, 4):
        kv_wait(slot)
        for p, copies in forwards[slot].items():
            @pl.when(place == p)
            def _():
                for c in copies:
                    c.start()
        split_heads(slot)
        send_e(1, slot, at(1)).wait_recv()
        if slot < 3:
            @pl.loop(0, 8)
            def _(i):
                chunk(slot, i)

    lane8 = lax.broadcasted_iota(jnp.int32, (8, tile), 0)

    def den_rows(fc):
        total = None
        for h in range(HEADS):
            pick = jnp.where(lane8 == h, 1.0, 0.0).astype(jnp.float32)
            term = lax.dot_general(
                pick, denacc[h, fc], (((1,), (1,)), ((), ())),
                precision=HIGHEST, preferred_element_type=jnp.float32,
            )
            total = term if total is None else total + term
        return total

    def n_copy(j):
        return [
            remote(sendbuf.at[j], nrecv.at[j], n_send.at[j], n_recv.at[j], (b, place_at(j))),
            remote(dsend.at[j], drecv.at[j], d_send.at[j], d_recv.at[j], (b, place_at(j))),
        ]

    @pl.loop(0, 8)
    def _(j):
        fc = place_at(j)
        chunk(3, fc)
        dsend[j] = den_rows(fc)
        sendbuf[j] = numacc[fc].astype(jnp.bfloat16)

        @pl.when(j > 0)
        def _():
            for c in n_copy(j - 1):
                c.start()

    den = dsend[7]
    for j in range(7):
        for c in n_copy(j):
            c.wait_recv()
        numacc[f] += nrecv[j].astype(jnp.float32)
        den = den + drecv[j]
    inverse = 1.0 / jnp.sqrt(1.0 + den)
    r8 = lax.broadcasted_iota(jnp.int32, (8, feat), 0)
    c8 = lax.broadcasted_iota(jnp.int32, (8, feat), 1)
    spread_of = jnp.where(r8 == c8 // dh, 1.0, 0.0).astype(jnp.float32)
    spread = lax.dot_general(
        inverse, spread_of, (((0,), (0,)), ((), ())),
        precision=HIGHEST, preferred_element_type=jnp.float32,
    )
    out[...] = (numacc[f] * spread).astype(jnp.bfloat16)

    for c in own_q + other_q + [inv_copy]:
        c.wait_send()
    for p in range(4):
        @pl.when(place == p)
        def _():
            for c in sends[p]:
                c.wait_send()

    @pl.when(place == 1)
    def _():
        for c in relays:
            c.wait_send()

    for slot in range(1, 4):
        for p, copies in forwards[slot].items():
            @pl.when(place == p)
            def _():
                for c in copies:
                    c.wait_send()
    for j in range(7):
        for c in n_copy(j):
            c.wait_send()


def on_device(queries, keys, values, tiles, edges):
    rows, feat = queries.shape
    stops, cap, tile = edges.shape[2], edges.shape[3], edges.shape[4]
    bf, f32, i32 = jnp.bfloat16, jnp.float32, jnp.int32
    dma = pltpu.SemaphoreType.DMA
    ebuf = pltpu.VMEM((cap, tile, tile), bf)
    any_spec = pl.BlockSpec(memory_space=pl.ANY)
    return pl.pallas_call(
        kernel,
        out_shape=jax.ShapeDtypeStruct((rows, feat), bf),
        in_specs=[pl.BlockSpec(memory_space=pltpu.SMEM)] + [any_spec] * 4,
        out_specs=pl.BlockSpec(memory_space=pltpu.VMEM),
        scratch_shapes=[
            pltpu.VMEM((8, rows, feat), bf),
            pltpu.VMEM((4, 2, rows, feat), bf),
            ebuf, ebuf, ebuf, ebuf, ebuf, ebuf,
            pltpu.VMEM((2, rows, feat), bf),
            pltpu.VMEM((2, 8, 128), i32),
            pltpu.SMEM((2, 8, 128), i32),
            pltpu.VMEM((HEADS, rows, feat // 2), bf),
            pltpu.VMEM((HEADS, rows, feat // 2), bf),
            pltpu.VMEM((rows, rows), f32),
            pltpu.VMEM((8, rows, feat), f32),
            pltpu.VMEM((HEADS, 8, rows, tile), f32),
            pltpu.VMEM((8, rows, feat), bf),
            pltpu.VMEM((8, 8, rows), f32),
            pltpu.VMEM((7, rows, feat), bf),
            pltpu.VMEM((7, 8, rows), f32),
            dma((5,)), dma((7,)), dma((7,)), dma((4,)), dma((4,)),
            dma((2, 2)), dma((4, 2)), dma((2, 2)),
            dma((4,)), dma((4,)), dma((2,)),
            dma((7,)), dma((7,)), dma((7,)), dma((7,)),
        ],
        compiler_params=pltpu.CompilerParams(collective_id=0, has_side_effects=True),
    )(tiles.reshape(stops, cap), queries, keys, values, edges.reshape(stops, cap, tile, tile))


def solution(mesh):
    return jax.shard_map(
        on_device,
        mesh=mesh,
        in_specs=(
            P(("blk", "fiber"), None),
            P(("blk", "fiber"), None),
            P(("blk", "fiber"), None),
            P("blk", "fiber", None, None),
            P("blk", "fiber", None, None, None, None),
        ),
        out_specs=P(("blk", "fiber"), None),
        check_vma=False,
    )
```

```python
import functools

import jax
import jax.numpy as jnp
from jax import lax
from jax.experimental import pallas as pl
from jax.experimental.pallas import tpu as pltpu
from jax.sharding import PartitionSpec as P

HEADS = 4
LEAKY_SLOPE = 0.2
PARTS = 4
MESH = pl.DeviceIdType.MESH

ORDER = [(2, 1), (2, 0), (1, 1), (1, 0), (3, 1), (3, 0), (0, 1), (0, 0)]
PLACE = {d: j for j, d in enumerate(ORDER)}


def kernel(
    tiles, lists, q_hbm, k_hbm, v_hbm, e_hbm, out,
    q_all, kv0, kv1, kv2, kv3, e0, e1, e2, e3, er1, er2, kvr, inv_v, inv_s,
    vturn, wtile, dtile, numacc, sendbuf, dsend, nrecv, drecv,
    local_sem, q_send, q_recv, e_send, e_recv, kv_send, kv_recv, kvf_send,
    relay_send, relay_recv, inv_sem, n_send, n_recv, d_send, d_recv,
):
    blocks = lax.axis_size("blk")
    b = lax.axis_index("blk")
    f = lax.axis_index("fiber")
    place = b % 4
    y = f // 2
    xh = f % 2
    even = place % 2 == 0
    stops, cap, tile, _ = e_hbm.shape
    q_tiles, _, feat = k_hbm.shape
    rows = q_tiles * tile
    dh = feat // HEADS
    scale = float(dh ** -0.5 * (stops * 8 * rows / 4) ** -0.5)
    ebufs = (e0, e1, e2, e3)
    kvs = (kv0, kv1, kv2, kv3)

    def at(db, flip=False):
        fb = 1 - xh if flip else xh
        return ((b + db + blocks) % blocks, y * 2 + fb)

    def fiber_at(dy, dx):
        return ((y + dy) % 4) * 2 + (xh + dx) % 2

    def place_at(j):
        k = j // 2
        dy = jnp.where(k == 0, 2, jnp.where(k == 1, 1, jnp.where(k == 2, 3, 0)))
        return fiber_at(dy, 1 - j % 2)

    def remote(src, dst, ssem, rsem, dev):
        return pltpu.make_async_remote_copy(
            src_ref=src, dst_ref=dst, send_sem=ssem, recv_sem=rsem,
            device_id=dev, device_id_type=MESH,
        )

    def share(fb):
        return q_all.at[pl.ds(fb * q_tiles, q_tiles)]

    locals_ = [
        pltpu.make_async_copy(q_hbm, share(f), local_sem.at[0]),
        pltpu.make_async_copy(k_hbm, kv0.at[0], local_sem.at[1]),
        pltpu.make_async_copy(v_hbm, kv0.at[1], local_sem.at[2]),
        pltpu.make_async_copy(e_hbm.at[0], e0, local_sem.at[3]),
    ]
    for c in locals_:
        c.start()

    barrier = pltpu.get_barrier_semaphore()
    partners = [at(d) for d in (-4, -3, -2, -1, 1, 2, 3, 4)]
    partners += [at(d, True) for d in (-2, -1, 1, 2)]
    partners += [(b, fiber_at(dy, dx)) for dy, dx in ORDER[:-1]]
    for dev in partners:
        pl.semaphore_signal(barrier, 1, device_id=dev, device_id_type=MESH)

    lane = lax.broadcasted_iota(jnp.int32, (8, 128), 1)
    row = lax.broadcasted_iota(jnp.int32, (8, 128), 0)
    slots = jnp.full((8, 128), cap, jnp.int32)
    for s in range(stops):
        for k in range(cap):
            slots = jnp.where((lane == tiles[s, k]) & (row == s), k, slots)
    inv_v[0, pl.ds(0, 8)] = slots
    inv_v[0, pl.ds(8, stops), pl.ds(0, cap)] = lists[...]
    for slot in range(stops):
        wtile[slot, cap] = jnp.zeros(wtile.shape[2:], wtile.dtype)
        dtile[slot, cap] = jnp.zeros(dtile.shape[2:], dtile.dtype)

    pl.semaphore_wait(barrier, len(partners))

    own_q = [
        remote(q_hbm, share(f), q_send.at[PLACE[d]], q_recv.at[PLACE[d]], (b, fiber_at(-d[0], d[1])))
        for d in ((0, 1), (3, 0), (1, 0), (2, 0))
    ]
    for c in own_q:
        c.start()
    pf = fiber_at(0, 1)
    inv_copy = remote(inv_v.at[0], inv_v.at[1], inv_sem.at[0], inv_sem.at[1], (b, pf))
    inv_copy.start()
    part = cap // PARTS

    def piece(ch):
        return pl.ds(ch * part, part)

    def one_e(s, slot, dev, ch):
        return remote(
            e_hbm.at[s, piece(ch)], ebufs[slot].at[piece(ch)],
            e_send.at[s, ch], e_recv.at[slot, ch], dev,
        )

    def send_e(s, slot, dev):
        return [one_e(s, slot, dev, ch) for ch in range(PARTS)]

    def send_kv(n, slot, dev):
        return [
            remote(k_hbm, kvs[slot].at[0], kv_send.at[n, 0], kv_recv.at[slot, 0], dev),
            remote(v_hbm, kvs[slot].at[1], kv_send.at[n, 1], kv_recv.at[slot, 1], dev),
        ]

    def to_relay(i):
        return [
            remote(
                e_hbm.at[i + 1, piece(ch)], (er1, er2)[i].at[piece(ch)],
                e_send.at[i + 1, ch], relay_recv.at[i, ch], at(-2, True),
            )
            for ch in range(PARTS)
        ]

    def kv_to_relay():
        return [
            remote((k_hbm, v_hbm)[i], kvr.at[i], kv_send.at[0, i], relay_recv.at[2, i], at(-2, True))
            for i in range(2)
        ]

    sends = {
        0: send_kv(1, 1, at(1)) + send_e(1, 1, at(1)),
        1: send_kv(1, 1, at(3)) + send_e(3, 1, at(3)),
        2: send_kv(1, 1, at(1)) + send_e(1, 1, at(1)),
        3: send_kv(1, 3, at(3)) + send_e(3, 3, at(3)),
    }
    late = {
        0: send_kv(0, 2, at(2)) + send_e(2, 2, at(2)) + send_e(3, 3, at(3)),
        1: send_kv(0, 1, at(1, True)) + send_e(1, 1, at(1, True)) + send_e(2, 2, at(2, True)),
        2: send_kv(0, 3, at(2)) + send_e(3, 2, at(3)) + send_e(2, 3, at(2)),
        3: kv_to_relay() + to_relay(0) + to_relay(1),
    }
    for p in range(4):
        @pl.when(place == p)
        def _():
            for c in sends[p]:
                c.start()

    remote(q_hbm, share(pf), q_send.at[6], q_recv.at[6], (b, pf)).wait_recv()
    other_q = [
        remote(share(pf), share(pf), q_send.at[PLACE[d]], q_recv.at[PLACE[d]], (b, fiber_at(-d[0], 0)))
        for d in ((3, 1), (1, 1), (2, 1))
    ]
    for c in other_q:
        c.start()
    for p in range(4):
        @pl.when(place == p)
        def _():
            for c in late[p]:
                c.start()

    inv_copy.wait_recv()
    inv_local = pltpu.make_async_copy(inv_v, inv_s, local_sem.at[4])
    inv_local.start()

    def relay_e(i, ch):
        slot, dev = ((2, at(3)), (3, at(4)))[i]
        return remote(
            (er1, er2)[i].at[piece(ch)], ebufs[slot].at[piece(ch)],
            relay_send.at[i, ch], e_recv.at[slot, ch], dev,
        )

    def relay_kv(i):
        return remote(kvr.at[i], kv2.at[i], relay_send.at[2, i], kv_recv.at[2, i], at(3))

    def pass_on(i):
        for ch in range(PARTS):
            to_relay(i)[ch].wait_recv()
            relay_e(i, ch).start()

    @pl.when(place == 1)
    def _():
        for i in range(2):
            kv_to_relay()[i].wait_recv()
            relay_kv(i).start()
        pass_on(0)

    for c in locals_:
        c.wait()
    inv_local.wait()

    stop_of = [
        jnp.int32(0),
        jnp.where(place == 0, 3, 1),
        jnp.where(place == 0, 1, jnp.where(place == 1, 3, 2)),
        jnp.where(place <= 1, 2, 3),
    ]
    from_partner = [
        jnp.int32(0),
        jnp.where(place == 2, 1, 0),
        jnp.where((place == 3) | (place == 0), 1, 0),
        jnp.where(place == 1, 1, 0),
    ]

    def slot_group(slot, first):
        def score_of(k, pair):
            t = jnp.maximum(inv_s[from_partner[slot], 8 + stop_of[slot], k], 0)
            r = lax.shift_right_logical(t, 1)
            c = lax.bitwise_and(t, 1)
            cols = pl.ds(pair * 2 * dh, 2 * dh)
            q = q_all[r, :, cols]
            zero = jnp.zeros_like(q)
            q2 = jnp.concatenate([jnp.where(low, q, zero), jnp.where(low, zero, q)], axis=0)
            key = kvs[slot][0, c, :, cols]
            return lax.dot_general(
                key, q2, (((1,), (1,)), ((), ())), preferred_element_type=jnp.float32
            )

        def edge_of(k):
            edge = (ebufs[slot][k].astype(jnp.float32) * scale).T
            return jnp.concatenate([edge, edge], axis=1)

        items = [(first + i, pair) for i in range(part) for pair in range(HEADS // 2)]
        score = score_of(*items[0])
        for i, (k, pair) in enumerate(items):
            now = score
            if i + 1 < len(items):
                score = score_of(*items[i + 1])
            if pair == 0:
                edge = edge_of(k)
            w = jnp.maximum(now, LEAKY_SLOPE * now) * edge
            sq = jnp.sum((w * w).reshape(tile // 8, 8, 2 * tile), axis=0)
            w = w.astype(jnp.bfloat16)
            for hh in range(2):
                wtile[slot, k, pair * 2 + hh] = w[:, hh * tile:(hh + 1) * tile]
                dtile[slot, k, pair * 2 + hh] = sq[:, hh * tile:(hh + 1) * tile]

    low = lax.broadcasted_iota(jnp.int32, (tile, 2 * dh), 1) < dh

    def weights(slot):
        vturn[:, pl.ds(slot * rows, rows)] = kvs[slot][1].reshape(rows, feat).T

        @pl.loop(0, PARTS)
        def _(ch):
            if slot > 0:
                one_e(1, slot, at(1), ch).wait_recv()
            slot_group(slot, ch * part)

    def chunk(fc, num, den):
        code = [
            [
                inv_s[from_partner[slot], stop_of[slot], fc * 4 + (rr * 2 + c)]
                for slot in range(stops)
                for c in range(2)
            ]
            for rr in range(2)
        ]
        for h in range(HEADS):
            w = jnp.concatenate(
                [
                    jnp.concatenate([wtile[i // 2, code[rr][i], h] for rr in range(2)], axis=1)
                    for i in range(2 * stops)
                ],
                axis=0,
            )
            feats = pl.ds(h * dh, dh)
            num[feats] = jnp.dot(
                vturn[feats, :], w, preferred_element_type=jnp.float32
            ).astype(num.dtype)
            for rr in range(2):
                sq = sum(dtile[i // 2, code[rr][i], h] for i in range(2 * stops))
                den[pl.ds(h, 1), pl.ds(rr * tile, tile)] = jnp.sum(sq, axis=0, keepdims=True)

    for j in range(6):
        fc = place_at(j)
        remote(q_hbm, share(fc), q_send.at[j], q_recv.at[j], (b, pf)).wait_recv()
    weights(0)

    @pl.when(place == 1)
    def _():
        pass_on(1)

    def kv_wait(slot):
        for c in send_kv(0, slot, at(1)):
            c.wait_recv()

    def kv_forward(n, slot, to):
        return [
            remote(kvs[slot].at[i], kvs[to].at[i], kvf_send.at[n, i], kv_recv.at[to, i], at(1))
            for i in range(2)
        ]

    forwards = {
        1: {2: kv_forward(0, 1, 2)},
        2: {0: kv_forward(0, 2, 3), 2: kv_forward(1, 2, 3)},
        3: {0: kv_forward(1, 3, 2)},
    }
    for slot in range(1, 4):
        for arrived in {1: (1,), 2: (2, 3), 3: ()}[slot]:
            kv_wait(arrived)
            for p, copies in forwards[arrived].items():
                @pl.when(place == p)
                def _():
                    for c in copies:
                        c.start()
        weights(slot)

    def n_copy(j):
        return [
            remote(sendbuf.at[j], nrecv.at[j], n_send.at[j], n_recv.at[j], (b, place_at(j))),
            remote(dsend.at[j], drecv.at[j], d_send.at[j], d_recv.at[j], (b, place_at(j))),
        ]

    @pl.loop(0, 7)
    def _(j):
        chunk(place_at(j), sendbuf.at[j], dsend.at[j])

        @pl.when(j > 0)
        def _():
            for c in n_copy(j - 1):
                c.start()

    chunk(f, numacc, dsend.at[7])
    for c in n_copy(6):
        c.start()

    den = dsend[7]
    for j in range(7):
        for c in n_copy(j):
            c.wait_recv()
        numacc[...] += nrecv[j].astype(jnp.float32)
        den = den + drecv[j]
    inverse = 1.0 / jnp.sqrt(1.0 + den)
    for h in range(HEADS):
        feats = pl.ds(h * dh, dh)
        sendbuf[7, feats] = (numacc[feats] * inverse[h:h + 1]).astype(jnp.bfloat16)
    out[...] = sendbuf[7].T

    for c in own_q + other_q + [inv_copy]:
        c.wait_send()
    for p in range(4):
        @pl.when(place == p)
        def _():
            for c in sends[p] + late[p]:
                c.wait_send()

    @pl.when(place == 1)
    def _():
        for i in range(2):
            relay_kv(i).wait_send()
            for ch in range(PARTS):
                relay_e(i, ch).wait_send()

    for slot in range(1, 4):
        for p, copies in forwards[slot].items():
            @pl.when(place == p)
            def _():
                for c in copies:
                    c.wait_send()
    for j in range(7):
        for c in n_copy(j):
            c.wait_send()


def on_device(queries, keys, values, tiles, edges):
    rows, feat = queries.shape
    stops, cap, tile = edges.shape[2], edges.shape[3], edges.shape[4]
    bf, f32, i32 = jnp.bfloat16, jnp.float32, jnp.int32
    dma = pltpu.SemaphoreType.DMA
    ebuf = pltpu.VMEM((cap, tile, tile), bf)
    kvbuf = pltpu.VMEM((2, rows // tile, tile, feat), bf)
    split = (rows // tile, tile, feat)
    lists = tiles.reshape(stops, cap)
    any_spec = pl.BlockSpec(memory_space=pl.ANY)
    return pl.pallas_call(
        kernel,
        out_shape=jax.ShapeDtypeStruct((rows, feat), bf),
        in_specs=[pl.BlockSpec(memory_space=pltpu.SMEM), pl.BlockSpec(memory_space=pltpu.VMEM)] + [any_spec] * 4,
        out_specs=pl.BlockSpec(memory_space=pltpu.VMEM),
        scratch_shapes=[
            pltpu.VMEM((8 * rows // tile, tile, feat), bf),
            kvbuf, kvbuf, kvbuf, kvbuf,
            ebuf, ebuf, ebuf, ebuf, ebuf, ebuf,
            kvbuf,
            pltpu.VMEM((2, 16, 128), i32),
            pltpu.SMEM((2, 16, 128), i32),
            pltpu.VMEM((feat, stops * rows), bf),
            pltpu.VMEM((stops, cap + 1, HEADS, tile, tile), bf),
            pltpu.VMEM((stops, cap + 1, HEADS, 8, tile), f32),
            pltpu.VMEM((feat, rows), f32),
            pltpu.VMEM((8, feat, rows), bf),
            pltpu.VMEM((8, HEADS, rows), f32),
            pltpu.VMEM((7, feat, rows), bf),
            pltpu.VMEM((7, HEADS, rows), f32),
            dma((5,)), dma((7,)), dma((7,)), dma((4, PARTS)), dma((4, PARTS)),
            dma((2, 2)), dma((4, 2)), dma((2, 2)),
            dma((3, PARTS)), dma((3, PARTS)), dma((2,)),
            dma((7,)), dma((7,)), dma((7,)), dma((7,)),
        ],
        compiler_params=pltpu.CompilerParams(collective_id=0, has_side_effects=True),
    )(
        lists, lists, queries.reshape(split), keys.reshape(split), values.reshape(split),
        edges.reshape(stops, cap, tile, tile),
    )


def solution(mesh):
    return jax.shard_map(
        on_device,
        mesh=mesh,
        in_specs=(
            P(("blk", "fiber"), None),
            P(("blk", "fiber"), None),
            P(("blk", "fiber"), None),
            P("blk", "fiber", None, None),
            P("blk", "fiber", None, None, None, None),
        ),
        out_specs=P(("blk", "fiber"), None),
        check_vma=False,
    )
```

```python
import functools

import jax
import jax.numpy as jnp
from jax import lax
from jax.experimental import pallas as pl
from jax.experimental.pallas import tpu as pltpu
from jax.sharding import PartitionSpec as P

HEADS = 4
LEAKY_SLOPE = 0.2
PARTS = 4
MESH = pl.DeviceIdType.MESH

ORDER = [(2, 1), (2, 0), (1, 1), (1, 0), (3, 1), (3, 0), (0, 1), (0, 0)]
PLACE = {d: j for j, d in enumerate(ORDER)}


def kernel(
    tiles, lists, q_hbm, k_hbm, v_hbm, e_hbm, out,
    q_all, kv0, kv1, kv2, kv3, e0, e1, e2, e3, er1, er2, kvr, inv_v, inv_s,
    vturn, wtile, dtile, numacc, sendbuf, dsend, nrecv, drecv,
    local_sem, q_send, q_recv, e_send, e_recv, kv_send, kv_recv, kvf_send,
    relay_send, relay_recv, inv_sem, n_send, n_recv, d_send, d_recv,
):
    blocks = lax.axis_size("blk")
    b = lax.axis_index("blk")
    f = lax.axis_index("fiber")
    place = b % 4
    y = f // 2
    xh = f % 2
    even = place % 2 == 0
    stops, cap, tile, _ = e_hbm.shape
    q_tiles, _, feat = k_hbm.shape
    rows = q_tiles * tile
    dh = feat // HEADS
    scale = float(dh ** -0.5 * (stops * 8 * rows / 4) ** -0.5)
    ebufs = (e0, e1, e2, e3)
    kvs = (kv0, kv1, kv2, kv3)

    def at(db, flip=False):
        fb = 1 - xh if flip else xh
        return ((b + db + blocks) % blocks, y * 2 + fb)

    def fiber_at(dy, dx):
        return ((y + dy) % 4) * 2 + (xh + dx) % 2

    def place_at(j):
        k = j // 2
        dy = jnp.where(k == 0, 2, jnp.where(k == 1, 1, jnp.where(k == 2, 3, 0)))
        return fiber_at(dy, 1 - j % 2)

    def remote(src, dst, ssem, rsem, dev):
        return pltpu.make_async_remote_copy(
            src_ref=src, dst_ref=dst, send_sem=ssem, recv_sem=rsem,
            device_id=dev, device_id_type=MESH,
        )

    def share(fb):
        return q_all.at[pl.ds(fb * q_tiles, q_tiles)]

    locals_ = [
        pltpu.make_async_copy(q_hbm, share(f), local_sem.at[0]),
        pltpu.make_async_copy(k_hbm, kv0.at[0], local_sem.at[1]),
        pltpu.make_async_copy(v_hbm, kv0.at[1], local_sem.at[2]),
        pltpu.make_async_copy(e_hbm.at[0], e0, local_sem.at[3]),
    ]
    for c in locals_:
        c.start()

    barrier = pltpu.get_barrier_semaphore()
    partners = [at(d) for d in (-4, -3, -2, -1, 1, 2, 3, 4)]
    partners += [at(d, True) for d in (-2, -1, 1, 2)]
    partners += [(b, fiber_at(dy, dx)) for dy, dx in ((0, 1), (1, 0), (2, 0), (3, 0))]
    for dev in partners:
        pl.semaphore_signal(barrier, 1, device_id=dev, device_id_type=MESH)

    lane = lax.broadcasted_iota(jnp.int32, (8, 128), 1)
    row = lax.broadcasted_iota(jnp.int32, (8, 128), 0)
    slots = jnp.full((8, 128), cap, jnp.int32)
    for s in range(stops):
        for k in range(cap):
            slots = jnp.where((lane == tiles[s, k]) & (row == s), k, slots)
    inv_v[0, pl.ds(0, 8)] = slots
    inv_v[0, pl.ds(8, stops), pl.ds(0, cap)] = lists[...]
    for slot in range(stops):
        wtile[slot, cap] = jnp.zeros(wtile.shape[2:], wtile.dtype)
        dtile[slot, cap] = jnp.zeros(dtile.shape[2:], dtile.dtype)

    pl.semaphore_wait(barrier, len(partners))

    own_q = [
        remote(q_hbm, share(f), q_send.at[PLACE[d]], q_recv.at[PLACE[d]], (b, fiber_at(-d[0], d[1])))
        for d in ((0, 1), (3, 0), (1, 0), (2, 0))
    ]
    for c in own_q:
        c.start()
    pf = fiber_at(0, 1)
    inv_copy = remote(inv_v.at[0], inv_v.at[1], inv_sem.at[0], inv_sem.at[1], (b, pf))
    inv_copy.start()
    part = cap // PARTS

    def piece(ch):
        return pl.ds(ch * part, part)

    def one_e(s, slot, dev, ch):
        return remote(
            e_hbm.at[s, piece(ch)], ebufs[slot].at[piece(ch)],
            e_send.at[s, ch], e_recv.at[slot, ch], dev,
        )

    def send_e(s, slot, dev):
        return [one_e(s, slot, dev, ch) for ch in range(PARTS)]

    def send_kv(n, slot, dev):
        return [
            remote(k_hbm, kvs[slot].at[0], kv_send.at[n, 0], kv_recv.at[slot, 0], dev),
            remote(v_hbm, kvs[slot].at[1], kv_send.at[n, 1], kv_recv.at[slot, 1], dev),
        ]

    def to_relay(i):
        return [
            remote(
                e_hbm.at[i + 1, piece(ch)], (er1, er2)[i].at[piece(ch)],
                e_send.at[i + 1, ch], relay_recv.at[i, ch], at(-2, True),
            )
            for ch in range(PARTS)
        ]

    def kv_to_relay():
        return [
            remote((k_hbm, v_hbm)[i], kvr.at[i], kv_send.at[0, i], relay_recv.at[2, i], at(-2, True))
            for i in range(2)
        ]

    sends = {
        0: send_kv(1, 1, at(1)) + send_e(1, 1, at(1)),
        1: send_kv(1, 1, at(3)) + send_e(3, 1, at(3)),
        2: send_kv(1, 1, at(1)) + send_e(1, 1, at(1)),
        3: send_kv(1, 3, at(3)) + send_e(3, 3, at(3)) + kv_to_relay() + to_relay(0) + to_relay(1),
    }
    late = {
        0: send_kv(0, 2, at(2)) + send_e(2, 2, at(2)) + send_e(3, 3, at(3)),
        1: send_kv(0, 1, at(1, True)) + send_e(1, 1, at(1, True)) + send_e(2, 2, at(2, True)),
        2: send_kv(0, 3, at(2)) + send_e(2, 3, at(2)) + send_e(3, 2, at(3)),
        3: [],
    }
    for p in range(4):
        @pl.when(place == p)
        def _():
            for c in sends[p]:
                c.start()

    remote(q_hbm, share(pf), q_send.at[6], q_recv.at[6], (b, pf)).wait_recv()
    other_q = [
        remote(share(pf), share(pf), q_send.at[PLACE[d]], q_recv.at[PLACE[d]], (b, fiber_at(-d[0], 0)))
        for d in ((3, 1), (1, 1), (2, 1))
    ]
    for c in other_q:
        c.start()
    for p in range(4):
        @pl.when(place == p)
        def _():
            for c in late[p]:
                c.start()

    inv_copy.wait_recv()
    inv_local = pltpu.make_async_copy(inv_v, inv_s, local_sem.at[4])
    inv_local.start()

    def relay_e(i, ch):
        slot, dev = ((2, at(3)), (3, at(4)))[i]
        return remote(
            (er1, er2)[i].at[piece(ch)], ebufs[slot].at[piece(ch)],
            relay_send.at[i, ch], e_recv.at[slot, ch], dev,
        )

    def relay_kv(i):
        return remote(kvr.at[i], kv2.at[i], relay_send.at[2, i], kv_recv.at[2, i], at(3))

    def pass_on(i):
        for ch in range(PARTS):
            to_relay(i)[ch].wait_recv()
            relay_e(i, ch).start()

    @pl.when(place == 1)
    def _():
        for i in range(2):
            kv_to_relay()[i].wait_recv()
            relay_kv(i).start()
        pass_on(0)

    for c in locals_:
        c.wait()
    inv_local.wait()

    stop_of = [
        jnp.int32(0),
        jnp.where(place == 0, 3, 1),
        jnp.where(place == 0, 1, jnp.where(place == 1, 3, 2)),
        jnp.where(place <= 1, 2, 3),
    ]
    from_partner = [
        jnp.int32(0),
        jnp.where(place == 2, 1, 0),
        jnp.where((place == 3) | (place == 0), 1, 0),
        jnp.where(place == 1, 1, 0),
    ]

    def slot_group(slot, first):
        def score_of(k, pair):
            t = jnp.maximum(inv_s[from_partner[slot], 8 + stop_of[slot], k], 0)
            r = lax.shift_right_logical(t, 1)
            c = lax.bitwise_and(t, 1)
            cols = pl.ds(pair * 2 * dh, 2 * dh)
            q = q_all[r, :, cols]
            zero = jnp.zeros_like(q)
            q2 = jnp.concatenate([jnp.where(low, q, zero), jnp.where(low, zero, q)], axis=0)
            key = kvs[slot][0, c, :, cols]
            return lax.dot_general(
                key, q2, (((1,), (1,)), ((), ())), preferred_element_type=jnp.float32
            )

        def edge_of(k):
            edge = (ebufs[slot][k].astype(jnp.float32) * scale).T
            return jnp.concatenate([edge, edge], axis=1)

        items = [(first + i, pair) for i in range(part) for pair in range(HEADS // 2)]
        score = score_of(*items[0])
        for i, (k, pair) in enumerate(items):
            now = score
            if i + 1 < len(items):
                score = score_of(*items[i + 1])
            if pair == 0:
                edge = edge_of(k)
            w = jnp.maximum(now, LEAKY_SLOPE * now) * edge
            sq = jnp.sum((w * w).reshape(tile // 8, 8, 2 * tile), axis=0)
            w = w.astype(jnp.bfloat16)
            for hh in range(2):
                wtile[slot, k, pair * 2 + hh] = w[:, hh * tile:(hh + 1) * tile]
                dtile[slot, k, pair * 2 + hh] = sq[:, hh * tile:(hh + 1) * tile]

    low = lax.broadcasted_iota(jnp.int32, (tile, 2 * dh), 1) < dh

    def weights(*slots):
        for slot in slots:
            vturn[:, pl.ds(slot * rows, rows)] = kvs[slot][1].reshape(rows, feat).T

        @pl.loop(0, PARTS)
        def _(ch):
            for slot in slots:
                if slot > 0:
                    one_e(1, slot, at(1), ch).wait_recv()
                slot_group(slot, ch * part)

    def chunk(fc, num, den):
        code = [
            [
                inv_s[from_partner[slot], stop_of[slot], fc * 4 + (rr * 2 + c)]
                for slot in range(stops)
                for c in range(2)
            ]
            for rr in range(2)
        ]
        for h in range(HEADS):
            w = jnp.concatenate(
                [
                    jnp.concatenate([wtile[i // 2, code[rr][i], h] for rr in range(2)], axis=1)
                    for i in range(2 * stops)
                ],
                axis=0,
            )
            feats = pl.ds(h * dh, dh)
            num[feats] = jnp.dot(
                vturn[feats, :], w, preferred_element_type=jnp.float32
            ).astype(num.dtype)
            for rr in range(2):
                sq = sum(dtile[i // 2, code[rr][i], h] for i in range(2 * stops))
                den[pl.ds(h, 1), pl.ds(rr * tile, tile)] = jnp.sum(sq, axis=0, keepdims=True)

    for j in range(6):
        fc = place_at(j)
        remote(q_hbm, share(fc), q_send.at[j], q_recv.at[j], (b, pf)).wait_recv()
    weights(0)

    @pl.when(place == 1)
    def _():
        pass_on(1)

    def kv_wait(slot):
        for c in send_kv(0, slot, at(1)):
            c.wait_recv()

    def kv_forward(n, slot, to):
        return [
            remote(kvs[slot].at[i], kvs[to].at[i], kvf_send.at[n, i], kv_recv.at[to, i], at(1))
            for i in range(2)
        ]

    forwards = {
        1: {2: kv_forward(0, 1, 2)},
        2: {0: kv_forward(0, 2, 3), 2: kv_forward(1, 2, 3)},
        3: {0: kv_forward(1, 3, 2)},
    }
    for slots in ((1,), (2, 3)):
        for slot in slots:
            kv_wait(slot)
            for p, copies in forwards[slot].items():
                @pl.when(place == p)
                def _():
                    for c in copies:
                        c.start()
        weights(*slots)

    def n_copy(j):
        return [
            remote(sendbuf.at[j], nrecv.at[j], n_send.at[j], n_recv.at[j], (b, place_at(j))),
            remote(dsend.at[j], drecv.at[j], d_send.at[j], d_recv.at[j], (b, place_at(j))),
        ]

    @pl.loop(0, 7)
    def _(j):
        chunk(place_at(j), sendbuf.at[j], dsend.at[j])

        @pl.when(j > 0)
        def _():
            for c in n_copy(j - 1):
                c.start()

    chunk(f, numacc, dsend.at[7])
    for c in n_copy(6):
        c.start()

    den = dsend[7]
    for j in range(7):
        for c in n_copy(j):
            c.wait_recv()
        numacc[...] += nrecv[j].astype(jnp.float32)
        den = den + drecv[j]
    inverse = 1.0 / jnp.sqrt(1.0 + den)
    for h in range(HEADS):
        feats = pl.ds(h * dh, dh)
        sendbuf[7, feats] = (numacc[feats] * inverse[h:h + 1]).astype(jnp.bfloat16)
    out[...] = sendbuf[7].T

    for c in own_q + other_q + [inv_copy]:
        c.wait_send()
    for p in range(4):
        @pl.when(place == p)
        def _():
            for c in sends[p] + late[p]:
                c.wait_send()

    @pl.when(place == 1)
    def _():
        for i in range(2):
            relay_kv(i).wait_send()
            for ch in range(PARTS):
                relay_e(i, ch).wait_send()

    for slot in range(1, 4):
        for p, copies in forwards[slot].items():
            @pl.when(place == p)
            def _():
                for c in copies:
                    c.wait_send()
    for j in range(7):
        for c in n_copy(j):
            c.wait_send()


def on_device(queries, keys, values, tiles, edges):
    rows, feat = queries.shape
    stops, cap, tile = edges.shape[2], edges.shape[3], edges.shape[4]
    bf, f32, i32 = jnp.bfloat16, jnp.float32, jnp.int32
    dma = pltpu.SemaphoreType.DMA
    ebuf = pltpu.VMEM((cap, tile, tile), bf)
    kvbuf = pltpu.VMEM((2, rows // tile, tile, feat), bf)
    split = (rows // tile, tile, feat)
    lists = tiles.reshape(stops, cap)
    any_spec = pl.BlockSpec(memory_space=pl.ANY)
    return pl.pallas_call(
        kernel,
        out_shape=jax.ShapeDtypeStruct((rows, feat), bf),
        in_specs=[pl.BlockSpec(memory_space=pltpu.SMEM), pl.BlockSpec(memory_space=pltpu.VMEM)] + [any_spec] * 4,
        out_specs=pl.BlockSpec(memory_space=pltpu.VMEM),
        scratch_shapes=[
            pltpu.VMEM((8 * rows // tile, tile, feat), bf),
            kvbuf, kvbuf, kvbuf, kvbuf,
            ebuf, ebuf, ebuf, ebuf, ebuf, ebuf,
            kvbuf,
            pltpu.VMEM((2, 16, 128), i32),
            pltpu.SMEM((2, 16, 128), i32),
            pltpu.VMEM((feat, stops * rows), bf),
            pltpu.VMEM((stops, cap + 1, HEADS, tile, tile), bf),
            pltpu.VMEM((stops, cap + 1, HEADS, 8, tile), f32),
            pltpu.VMEM((feat, rows), f32),
            pltpu.VMEM((8, feat, rows), bf),
            pltpu.VMEM((8, HEADS, rows), f32),
            pltpu.VMEM((7, feat, rows), bf),
            pltpu.VMEM((7, HEADS, rows), f32),
            dma((5,)), dma((7,)), dma((7,)), dma((4, PARTS)), dma((4, PARTS)),
            dma((2, 2)), dma((4, 2)), dma((2, 2)),
            dma((3, PARTS)), dma((3, PARTS)), dma((2,)),
            dma((7,)), dma((7,)), dma((7,)), dma((7,)),
        ],
        compiler_params=pltpu.CompilerParams(collective_id=0, has_side_effects=True),
    )(
        lists, lists, queries.reshape(split), keys.reshape(split), values.reshape(split),
        edges.reshape(stops, cap, tile, tile),
    )


def solution(mesh):
    return jax.shard_map(
        on_device,
        mesh=mesh,
        in_specs=(
            P(("blk", "fiber"), None),
            P(("blk", "fiber"), None),
            P(("blk", "fiber"), None),
            P("blk", "fiber", None, None),
            P("blk", "fiber", None, None, None, None),
        ),
        out_specs=P(("blk", "fiber"), None),
        check_vma=False,
    )
```

```python
import functools

import jax
import jax.numpy as jnp
from jax import lax
from jax.experimental import pallas as pl
from jax.experimental.pallas import tpu as pltpu
from jax.sharding import PartitionSpec as P

HEADS = 4
LEAKY_SLOPE = 0.2
PARTS = 4
MESH = pl.DeviceIdType.MESH

ORDER = [(2, 1), (2, 0), (1, 1), (1, 0), (3, 1), (3, 0), (0, 1), (0, 0)]
PLACE = {d: j for j, d in enumerate(ORDER)}


def kernel(
    tiles, lists, q_hbm, k_hbm, v_hbm, e_hbm, out,
    q_all, kv0, kv1, kv2, kv3, e0, e1, e2, e3, er1, er2, kvr, inv_v, inv_s,
    vturn, eturn, wtile, dtile, numacc, sendbuf, dsend, nrecv, drecv,
    local_sem, q_send, q_recv, e_send, e_recv, kv_send, kv_recv, kvf_send,
    relay_send, relay_recv, inv_sem, n_send, n_recv, d_send, d_recv,
):
    blocks = lax.axis_size("blk")
    b = lax.axis_index("blk")
    f = lax.axis_index("fiber")
    place = b % 4
    y = f // 2
    xh = f % 2
    even = place % 2 == 0
    stops, cap, tile, _ = e_hbm.shape
    q_tiles, _, feat = k_hbm.shape
    rows = q_tiles * tile
    dh = feat // HEADS
    scale = float(dh ** -0.5 * (stops * 8 * rows / 4) ** -0.5)
    ebufs = (e0, e1, e2, e3)
    kvs = (kv0, kv1, kv2, kv3)

    def at(db, flip=False):
        fb = 1 - xh if flip else xh
        return ((b + db + blocks) % blocks, y * 2 + fb)

    def fiber_at(dy, dx):
        return ((y + dy) % 4) * 2 + (xh + dx) % 2

    def place_at(j):
        k = j // 2
        dy = jnp.where(k == 0, 2, jnp.where(k == 1, 1, jnp.where(k == 2, 3, 0)))
        return fiber_at(dy, 1 - j % 2)

    def remote(src, dst, ssem, rsem, dev):
        return pltpu.make_async_remote_copy(
            src_ref=src, dst_ref=dst, send_sem=ssem, recv_sem=rsem,
            device_id=dev, device_id_type=MESH,
        )

    def share(fb):
        return q_all.at[pl.ds(fb * q_tiles, q_tiles)]

    locals_ = [
        pltpu.make_async_copy(q_hbm, share(f), local_sem.at[0]),
        pltpu.make_async_copy(k_hbm, kv0.at[0], local_sem.at[1]),
        pltpu.make_async_copy(v_hbm, kv0.at[1], local_sem.at[2]),
        pltpu.make_async_copy(e_hbm.at[0], e0, local_sem.at[3]),
    ]
    for c in locals_:
        c.start()

    barrier = pltpu.get_barrier_semaphore()
    partners = [at(d) for d in (-4, -3, -2, -1, 1, 2, 3, 4)]
    partners += [at(d, True) for d in (-2, -1, 1, 2)]
    partners += [(b, fiber_at(dy, dx)) for dy, dx in ((0, 1), (1, 0), (2, 0), (3, 0))]
    for dev in partners:
        pl.semaphore_signal(barrier, 1, device_id=dev, device_id_type=MESH)

    lane = lax.broadcasted_iota(jnp.int32, (8, 128), 1)
    row = lax.broadcasted_iota(jnp.int32, (8, 128), 0)
    slots = jnp.full((8, 128), cap, jnp.int32)
    for s in range(stops):
        for k in range(cap):
            slots = jnp.where((lane == tiles[s, k]) & (row == s), k, slots)
    inv_v[0, pl.ds(0, 8)] = slots
    inv_v[0, pl.ds(8, stops), pl.ds(0, cap)] = lists[...]
    for slot in range(stops):
        wtile[slot, cap] = jnp.zeros(wtile.shape[2:], wtile.dtype)
        dtile[slot, cap] = jnp.zeros(dtile.shape[2:], dtile.dtype)

    pl.semaphore_wait(barrier, len(partners))

    own_q = [
        remote(q_hbm, share(f), q_send.at[PLACE[d]], q_recv.at[PLACE[d]], (b, fiber_at(-d[0], d[1])))
        for d in ((0, 1), (3, 0), (1, 0), (2, 0))
    ]
    for c in own_q:
        c.start()
    pf = fiber_at(0, 1)
    inv_copy = remote(inv_v.at[0], inv_v.at[1], inv_sem.at[0], inv_sem.at[1], (b, pf))
    inv_copy.start()
    part = cap // PARTS

    def piece(ch):
        return pl.ds(ch * part, part)

    def one_e(s, slot, dev, ch):
        return remote(
            e_hbm.at[s, piece(ch)], ebufs[slot].at[piece(ch)],
            e_send.at[s, ch], e_recv.at[slot, ch], dev,
        )

    def send_e(s, slot, dev):
        return [one_e(s, slot, dev, ch) for ch in range(PARTS)]

    def send_kv(n, slot, dev):
        return [
            remote(k_hbm, kvs[slot].at[0], kv_send.at[n, 0], kv_recv.at[slot, 0], dev),
            remote(v_hbm, kvs[slot].at[1], kv_send.at[n, 1], kv_recv.at[slot, 1], dev),
        ]

    def to_relay(i):
        return [
            remote(
                e_hbm.at[i + 1, piece(ch)], (er1, er2)[i].at[piece(ch)],
                e_send.at[i + 1, ch], relay_recv.at[i, ch], at(-2, True),
            )
            for ch in range(PARTS)
        ]

    def kv_to_relay():
        return [
            remote((k_hbm, v_hbm)[i], kvr.at[i], kv_send.at[0, i], relay_recv.at[2, i], at(-2, True))
            for i in range(2)
        ]

    sends = {
        0: send_kv(1, 1, at(1)) + send_e(1, 1, at(1)),
        1: send_kv(1, 1, at(3)) + send_e(3, 1, at(3)),
        2: send_kv(1, 1, at(1)) + send_e(1, 1, at(1)),
        3: send_kv(1, 3, at(3)) + send_e(3, 3, at(3)) + kv_to_relay() + to_relay(0) + to_relay(1),
    }
    late = {
        0: send_kv(0, 2, at(2)) + send_e(2, 2, at(2)) + send_e(3, 3, at(3)),
        1: send_kv(0, 1, at(1, True)) + send_e(1, 1, at(1, True)) + send_e(2, 2, at(2, True)),
        2: send_kv(0, 3, at(2)) + send_e(2, 3, at(2)) + send_e(3, 2, at(3)),
        3: [],
    }
    for p in range(4):
        @pl.when(place == p)
        def _():
            for c in sends[p]:
                c.start()

    remote(q_hbm, share(pf), q_send.at[6], q_recv.at[6], (b, pf)).wait_recv()
    other_q = [
        remote(share(pf), share(pf), q_send.at[PLACE[d]], q_recv.at[PLACE[d]], (b, fiber_at(-d[0], 0)))
        for d in ((3, 1), (1, 1), (2, 1))
    ]
    for c in other_q:
        c.start()
    for p in range(4):
        @pl.when(place == p)
        def _():
            for c in late[p]:
                c.start()

    inv_copy.wait_recv()
    inv_local = pltpu.make_async_copy(inv_v, inv_s, local_sem.at[4])
    inv_local.start()

    def relay_e(i, ch):
        slot, dev = ((2, at(3)), (3, at(4)))[i]
        return remote(
            (er1, er2)[i].at[piece(ch)], ebufs[slot].at[piece(ch)],
            relay_send.at[i, ch], e_recv.at[slot, ch], dev,
        )

    def relay_kv(i):
        return remote(kvr.at[i], kv2.at[i], relay_send.at[2, i], kv_recv.at[2, i], at(3))

    def pass_on(i):
        for ch in range(PARTS):
            to_relay(i)[ch].wait_recv()
            relay_e(i, ch).start()

    @pl.when(place == 1)
    def _():
        for i in range(2):
            kv_to_relay()[i].wait_recv()
            relay_kv(i).start()
        pass_on(0)

    for c in locals_:
        c.wait()
    inv_local.wait()

    stop_of = [
        jnp.int32(0),
        jnp.where(place == 0, 3, 1),
        jnp.where(place == 0, 1, jnp.where(place == 1, 3, 2)),
        jnp.where(place <= 1, 2, 3),
    ]
    from_partner = [
        jnp.int32(0),
        jnp.where(place == 2, 1, 0),
        jnp.where((place == 3) | (place == 0), 1, 0),
        jnp.where(place == 1, 1, 0),
    ]

    def slot_group(slot, first):
        def score_of(k, pair):
            t = jnp.maximum(inv_s[from_partner[slot], 8 + stop_of[slot], k], 0)
            r = lax.shift_right_logical(t, 1)
            c = lax.bitwise_and(t, 1)
            cols = pl.ds(pair * 2 * dh, 2 * dh)
            q = q_all[r, :, cols]
            zero = jnp.zeros_like(q)
            q2 = jnp.concatenate([jnp.where(low, q, zero), jnp.where(low, zero, q)], axis=0)
            key = kvs[slot][0, c, :, cols]
            return lax.dot_general(
                key, q2, (((1,), (1,)), ((), ())), preferred_element_type=jnp.float32
            )

        def edge_of(k):
            edge = eturn[k] if slot == 0 else (ebufs[slot][k].astype(jnp.float32) * scale).T
            return jnp.concatenate([edge, edge], axis=1)

        items = [(first + i, pair) for i in range(part) for pair in range(HEADS // 2)]
        score = score_of(*items[0])
        for i, (k, pair) in enumerate(items):
            now = score
            if i + 1 < len(items):
                score = score_of(*items[i + 1])
            if pair == 0:
                edge = edge_of(k)
            w = jnp.maximum(now, LEAKY_SLOPE * now) * edge
            sq = jnp.sum((w * w).reshape(tile // 8, 8, 2 * tile), axis=0)
            w = w.astype(jnp.bfloat16)
            for hh in range(2):
                wtile[slot, k, pair * 2 + hh] = w[:, hh * tile:(hh + 1) * tile]
                dtile[slot, k, pair * 2 + hh] = sq[:, hh * tile:(hh + 1) * tile]

    low = lax.broadcasted_iota(jnp.int32, (tile, 2 * dh), 1) < dh

    def weights(*slots):
        for slot in slots:
            if slot > 0:
                vturn[:, pl.ds(slot * rows, rows)] = kvs[slot][1].reshape(rows, feat).T

        @pl.loop(0, PARTS)
        def _(ch):
            for slot in slots:
                if slot > 0:
                    one_e(1, slot, at(1), ch).wait_recv()
                slot_group(slot, ch * part)

    def chunk(fc, num, den):
        code = [
            [
                inv_s[from_partner[slot], stop_of[slot], fc * 4 + (rr * 2 + c)]
                for slot in range(stops)
                for c in range(2)
            ]
            for rr in range(2)
        ]
        for h in range(HEADS):
            w = jnp.concatenate(
                [
                    jnp.concatenate([wtile[i // 2, code[rr][i], h] for rr in range(2)], axis=1)
                    for i in range(2 * stops)
                ],
                axis=0,
            )
            feats = pl.ds(h * dh, dh)
            num[feats] = jnp.dot(
                vturn[feats, :], w, preferred_element_type=jnp.float32
            ).astype(num.dtype)
            for rr in range(2):
                sq = sum(dtile[i // 2, code[rr][i], h] for i in range(2 * stops))
                den[pl.ds(h, 1), pl.ds(rr * tile, tile)] = jnp.sum(sq, axis=0, keepdims=True)

    vturn[:, pl.ds(0, rows)] = kv0[1].reshape(rows, feat).T

    @pl.loop(0, cap // 4)
    def _(i):
        for k in range(4):
            eturn[4 * i + k] = (e0[4 * i + k].astype(jnp.float32) * scale).T

    for j in range(6):
        fc = place_at(j)
        remote(q_hbm, share(fc), q_send.at[j], q_recv.at[j], (b, pf)).wait_recv()
    weights(0)

    @pl.when(place == 1)
    def _():
        pass_on(1)

    def kv_wait(slot):
        for c in send_kv(0, slot, at(1)):
            c.wait_recv()

    def kv_forward(n, slot, to):
        return [
            remote(kvs[slot].at[i], kvs[to].at[i], kvf_send.at[n, i], kv_recv.at[to, i], at(1))
            for i in range(2)
        ]

    forwards = {
        1: {2: kv_forward(0, 1, 2)},
        2: {0: kv_forward(0, 2, 3), 2: kv_forward(1, 2, 3)},
        3: {0: kv_forward(1, 3, 2)},
    }
    for slots in ((1,), (2, 3)):
        for slot in slots:
            kv_wait(slot)
            for p, copies in forwards[slot].items():
                @pl.when(place == p)
                def _():
                    for c in copies:
                        c.start()
        weights(*slots)

    def n_copy(j):
        return [
            remote(sendbuf.at[j], nrecv.at[j], n_send.at[j], n_recv.at[j], (b, place_at(j))),
            remote(dsend.at[j], drecv.at[j], d_send.at[j], d_recv.at[j], (b, place_at(j))),
        ]

    @pl.loop(0, 7)
    def _(j):
        chunk(place_at(j), sendbuf.at[j], dsend.at[j])

        @pl.when(j > 0)
        def _():
            for c in n_copy(j - 1):
                c.start()

    chunk(f, numacc, dsend.at[7])
    for c in n_copy(6):
        c.start()

    den = dsend[7]
    for j in range(7):
        for c in n_copy(j):
            c.wait_recv()
        numacc[...] += nrecv[j].astype(jnp.float32)
        den = den + drecv[j]
    inverse = 1.0 / jnp.sqrt(1.0 + den)
    for h in range(HEADS):
        feats = pl.ds(h * dh, dh)
        sendbuf[7, feats] = (numacc[feats] * inverse[h:h + 1]).astype(jnp.bfloat16)
    out[...] = sendbuf[7].T

    for c in own_q + other_q + [inv_copy]:
        c.wait_send()
    for p in range(4):
        @pl.when(place == p)
        def _():
            for c in sends[p] + late[p]:
                c.wait_send()

    @pl.when(place == 1)
    def _():
        for i in range(2):
            relay_kv(i).wait_send()
            for ch in range(PARTS):
                relay_e(i, ch).wait_send()

    for slot in range(1, 4):
        for p, copies in forwards[slot].items():
            @pl.when(place == p)
            def _():
                for c in copies:
                    c.wait_send()
    for j in range(7):
        for c in n_copy(j):
            c.wait_send()


def on_device(queries, keys, values, tiles, edges):
    rows, feat = queries.shape
    stops, cap, tile = edges.shape[2], edges.shape[3], edges.shape[4]
    bf, f32, i32 = jnp.bfloat16, jnp.float32, jnp.int32
    dma = pltpu.SemaphoreType.DMA
    ebuf = pltpu.VMEM((cap, tile, tile), bf)
    kvbuf = pltpu.VMEM((2, rows // tile, tile, feat), bf)
    split = (rows // tile, tile, feat)
    lists = tiles.reshape(stops, cap)
    any_spec = pl.BlockSpec(memory_space=pl.ANY)
    return pl.pallas_call(
        kernel,
        out_shape=pltpu.VMEM((rows, feat), bf),
        in_specs=[pl.BlockSpec(memory_space=pltpu.SMEM), pl.BlockSpec(memory_space=pltpu.VMEM)] + [any_spec] * 4,
        out_specs=pl.BlockSpec(memory_space=pltpu.VMEM),
        scratch_shapes=[
            pltpu.VMEM((8 * rows // tile, tile, feat), bf),
            kvbuf, kvbuf, kvbuf, kvbuf,
            ebuf, ebuf, ebuf, ebuf, ebuf, ebuf,
            kvbuf,
            pltpu.VMEM((2, 16, 128), i32),
            pltpu.SMEM((2, 16, 128), i32),
            pltpu.VMEM((feat, stops * rows), bf),
            pltpu.VMEM((cap, tile, tile), f32),
            pltpu.VMEM((stops, cap + 1, HEADS, tile, tile), bf),
            pltpu.VMEM((stops, cap + 1, HEADS, 8, tile), f32),
            pltpu.VMEM((feat, rows), f32),
            pltpu.VMEM((8, feat, rows), bf),
            pltpu.VMEM((8, HEADS, rows), f32),
            pltpu.VMEM((7, feat, rows), bf),
            pltpu.VMEM((7, HEADS, rows), f32),
            dma((5,)), dma((7,)), dma((7,)), dma((4, PARTS)), dma((4, PARTS)),
            dma((2, 2)), dma((4, 2)), dma((2, 2)),
            dma((3, PARTS)), dma((3, PARTS)), dma((2,)),
            dma((7,)), dma((7,)), dma((7,)), dma((7,)),
        ],
        compiler_params=pltpu.CompilerParams(collective_id=0, has_side_effects=True),
    )(
        lists, lists, queries.reshape(split), keys.reshape(split), values.reshape(split),
        edges.reshape(stops, cap, tile, tile),
    )


def solution(mesh):
    return jax.shard_map(
        on_device,
        mesh=mesh,
        in_specs=(
            P(("blk", "fiber"), None),
            P(("blk", "fiber"), None),
            P(("blk", "fiber"), None),
            P("blk", "fiber", None, None),
            P("blk", "fiber", None, None, None, None),
        ),
        out_specs=P(("blk", "fiber"), None),
        check_vma=False,
    )
```

```python
import functools

import jax
import jax.numpy as jnp
from jax import lax
from jax.experimental import pallas as pl
from jax.experimental.pallas import tpu as pltpu
from jax.sharding import PartitionSpec as P

HEADS = 4
LEAKY_SLOPE = 0.2
PARTS = 4
MESH = pl.DeviceIdType.MESH

ORDER = [(2, 1), (2, 0), (1, 1), (1, 0), (3, 1), (3, 0), (0, 1), (0, 0)]
PLACE = {d: j for j, d in enumerate(ORDER)}


def kernel(
    tiles, lists, q_hbm, k_hbm, v_hbm, e_hbm, out,
    q_all, kv0, kv1, kv2, kv3, e0, e1, e2, e3, er1, er2, kvr, inv_v, inv_s,
    vturn, kmask, eturn, wtile, dtile, numacc, sendbuf, dsend, nrecv, drecv,
    local_sem, q_send, q_recv, e_send, e_recv, kv_send, kv_recv, kvf_send,
    relay_send, relay_recv, inv_sem, n_send, n_recv, d_send, d_recv,
):
    blocks = lax.axis_size("blk")
    b = lax.axis_index("blk")
    f = lax.axis_index("fiber")
    place = b % 4
    y = f // 2
    xh = f % 2
    even = place % 2 == 0
    stops, cap, tile, _ = e_hbm.shape
    q_tiles, _, feat = k_hbm.shape
    rows = q_tiles * tile
    dh = feat // HEADS
    scale = float(dh ** -0.5 * (stops * 8 * rows / 4) ** -0.5)
    ebufs = (e0, e1, e2, e3)
    kvs = (kv0, kv1, kv2, kv3)

    def at(db, flip=False):
        fb = 1 - xh if flip else xh
        return ((b + db + blocks) % blocks, y * 2 + fb)

    def fiber_at(dy, dx):
        return ((y + dy) % 4) * 2 + (xh + dx) % 2

    def place_at(j):
        k = j // 2
        dy = jnp.where(k == 0, 2, jnp.where(k == 1, 1, jnp.where(k == 2, 3, 0)))
        return fiber_at(dy, 1 - j % 2)

    def remote(src, dst, ssem, rsem, dev):
        return pltpu.make_async_remote_copy(
            src_ref=src, dst_ref=dst, send_sem=ssem, recv_sem=rsem,
            device_id=dev, device_id_type=MESH,
        )

    def share(fb):
        return q_all.at[pl.ds(fb * q_tiles, q_tiles)]

    locals_ = [
        pltpu.make_async_copy(q_hbm, share(f), local_sem.at[0]),
        pltpu.make_async_copy(k_hbm, kv0.at[0], local_sem.at[1]),
        pltpu.make_async_copy(v_hbm, kv0.at[1], local_sem.at[2]),
        pltpu.make_async_copy(e_hbm.at[0], e0, local_sem.at[3]),
    ]
    for c in locals_:
        c.start()

    barrier = pltpu.get_barrier_semaphore()
    partners = [at(d) for d in (-4, -3, -2, -1, 1, 2, 3, 4)]
    partners += [at(d, True) for d in (-2, -1, 1, 2)]
    partners += [(b, fiber_at(dy, dx)) for dy, dx in ((0, 1), (1, 0), (2, 0), (3, 0))]
    for dev in partners:
        pl.semaphore_signal(barrier, 1, device_id=dev, device_id_type=MESH)

    lane = lax.broadcasted_iota(jnp.int32, (8, 128), 1)
    row = lax.broadcasted_iota(jnp.int32, (8, 128), 0)
    slots = jnp.full((8, 128), cap, jnp.int32)
    for s in range(stops):
        for k in range(cap):
            slots = jnp.where((lane == tiles[s, k]) & (row == s), k, slots)
    inv_v[0, pl.ds(0, 8)] = slots
    inv_v[0, pl.ds(8, stops), pl.ds(0, cap)] = lists[...]
    for slot in range(stops):
        wtile[slot, cap] = jnp.zeros(wtile.shape[2:], wtile.dtype)
        dtile[slot, cap] = jnp.zeros(dtile.shape[2:], dtile.dtype)

    pl.semaphore_wait(barrier, len(partners))

    own_q = [
        remote(q_hbm, share(f), q_send.at[PLACE[d]], q_recv.at[PLACE[d]], (b, fiber_at(-d[0], d[1])))
        for d in ((0, 1), (3, 0), (1, 0), (2, 0))
    ]
    for c in own_q:
        c.start()
    pf = fiber_at(0, 1)
    inv_copy = remote(inv_v.at[0], inv_v.at[1], inv_sem.at[0], inv_sem.at[1], (b, pf))
    inv_copy.start()
    part = cap // PARTS

    def piece(ch):
        return pl.ds(ch * part, part)

    def one_e(s, slot, dev, ch):
        return remote(
            e_hbm.at[s, piece(ch)], ebufs[slot].at[piece(ch)],
            e_send.at[s, ch], e_recv.at[slot, ch], dev,
        )

    def send_e(s, slot, dev):
        return [one_e(s, slot, dev, ch) for ch in range(PARTS)]

    def send_kv(n, slot, dev):
        return [
            remote(k_hbm, kvs[slot].at[0], kv_send.at[n, 0], kv_recv.at[slot, 0], dev),
            remote(v_hbm, kvs[slot].at[1], kv_send.at[n, 1], kv_recv.at[slot, 1], dev),
        ]

    def to_relay(i):
        return [
            remote(
                e_hbm.at[i + 1, piece(ch)], (er1, er2)[i].at[piece(ch)],
                e_send.at[i + 1, ch], relay_recv.at[i, ch], at(-2, True),
            )
            for ch in range(PARTS)
        ]

    def kv_to_relay():
        return [
            remote((k_hbm, v_hbm)[i], kvr.at[i], kv_send.at[0, i], relay_recv.at[2, i], at(-2, True))
            for i in range(2)
        ]

    sends = {
        0: send_kv(1, 1, at(1)) + send_e(1, 1, at(1)),
        1: send_kv(1, 1, at(3)) + send_e(3, 1, at(3)),
        2: send_kv(1, 1, at(1)) + send_e(1, 1, at(1)),
        3: send_kv(1, 3, at(3)) + send_e(3, 3, at(3)) + kv_to_relay() + to_relay(0) + to_relay(1),
    }
    late = {
        0: send_kv(0, 2, at(2)) + send_e(2, 2, at(2)) + send_e(3, 3, at(3)),
        1: send_kv(0, 1, at(1, True)) + send_e(1, 1, at(1, True)) + send_e(2, 2, at(2, True)),
        2: send_kv(0, 3, at(2)) + send_e(2, 3, at(2)) + send_e(3, 2, at(3)),
        3: [],
    }
    for p in range(4):
        @pl.when(place == p)
        def _():
            for c in sends[p]:
                c.start()

    remote(q_hbm, share(pf), q_send.at[6], q_recv.at[6], (b, pf)).wait_recv()
    other_q = [
        remote(share(pf), share(pf), q_send.at[PLACE[d]], q_recv.at[PLACE[d]], (b, fiber_at(-d[0], 0)))
        for d in ((3, 1), (1, 1), (2, 1))
    ]
    for c in other_q:
        c.start()
    for p in range(4):
        @pl.when(place == p)
        def _():
            for c in late[p]:
                c.start()

    inv_copy.wait_recv()
    inv_local = pltpu.make_async_copy(inv_v, inv_s, local_sem.at[4])
    inv_local.start()

    def relay_e(i, ch):
        slot, dev = ((2, at(3)), (3, at(4)))[i]
        return remote(
            (er1, er2)[i].at[piece(ch)], ebufs[slot].at[piece(ch)],
            relay_send.at[i, ch], e_recv.at[slot, ch], dev,
        )

    def relay_kv(i):
        return remote(kvr.at[i], kv2.at[i], relay_send.at[2, i], kv_recv.at[2, i], at(3))

    def pass_on(i):
        for ch in range(PARTS):
            to_relay(i)[ch].wait_recv()
            relay_e(i, ch).start()

    @pl.when(place == 1)
    def _():
        for i in range(2):
            kv_to_relay()[i].wait_recv()
            relay_kv(i).start()
        pass_on(0)

    for c in locals_:
        c.wait()
    inv_local.wait()

    stop_of = [
        jnp.int32(0),
        jnp.where(place == 0, 3, 1),
        jnp.where(place == 0, 1, jnp.where(place == 1, 3, 2)),
        jnp.where(place <= 1, 2, 3),
    ]
    from_partner = [
        jnp.int32(0),
        jnp.where(place == 2, 1, 0),
        jnp.where((place == 3) | (place == 0), 1, 0),
        jnp.where(place == 1, 1, 0),
    ]

    def slot_group(slot, first):
        def score_of(k, pair):
            t = jnp.maximum(inv_s[from_partner[slot], 8 + stop_of[slot], k], 0)
            r = lax.shift_right_logical(t, 1)
            c = lax.bitwise_and(t, 1)
            cols = pl.ds(pair * 2 * dh, 2 * dh)
            return lax.dot_general(
                kmask[slot, c, pair], q_all[r, :, cols], (((1,), (1,)), ((), ())),
                preferred_element_type=jnp.float32,
            )

        def edge_of(k):
            edge = eturn[k] if slot == 0 else (ebufs[slot][k].astype(jnp.float32) * scale).T
            return jnp.concatenate([edge, edge], axis=0)

        items = [(first + i, pair) for i in range(part) for pair in range(HEADS // 2)]
        score = score_of(*items[0])
        for i, (k, pair) in enumerate(items):
            now = score
            if i + 1 < len(items):
                score = score_of(*items[i + 1])
            if pair == 0:
                edge = edge_of(k)
            w = jnp.maximum(now, LEAKY_SLOPE * now) * edge
            sq = jnp.sum((w * w).reshape(2, tile // 8, 8, tile), axis=1)
            w = w.astype(jnp.bfloat16)
            for hh in range(2):
                wtile[slot, k, pair * 2 + hh] = w[hh * tile:(hh + 1) * tile]
                dtile[slot, k, pair * 2 + hh] = sq[hh]

    low = lax.broadcasted_iota(jnp.int32, (tile, 2 * dh), 1) < dh

    def mask_keys(slot):
        for c in range(2):
            for pair in range(HEADS // 2):
                key = kvs[slot][0, c, :, pl.ds(pair * 2 * dh, 2 * dh)]
                zero = jnp.zeros_like(key)
                kmask[slot, c, pair] = jnp.concatenate(
                    [jnp.where(low, key, zero), jnp.where(low, zero, key)], axis=0
                )

    def weights(*slots):
        for slot in slots:
            if slot > 0:
                mask_keys(slot)
                vturn[:, pl.ds(slot * rows, rows)] = kvs[slot][1].reshape(rows, feat).T

        @pl.loop(0, PARTS)
        def _(ch):
            for slot in slots:
                if slot > 0:
                    one_e(1, slot, at(1), ch).wait_recv()
                slot_group(slot, ch * part)

    def chunk(fc, num, den):
        code = [
            [
                inv_s[from_partner[slot], stop_of[slot], fc * 4 + (rr * 2 + c)]
                for slot in range(stops)
                for c in range(2)
            ]
            for rr in range(2)
        ]
        for h in range(HEADS):
            w = jnp.concatenate(
                [
                    jnp.concatenate([wtile[i // 2, code[rr][i], h] for rr in range(2)], axis=1)
                    for i in range(2 * stops)
                ],
                axis=0,
            )
            feats = pl.ds(h * dh, dh)
            num[feats] = jnp.dot(
                vturn[feats, :], w, preferred_element_type=jnp.float32
            ).astype(num.dtype)
            for rr in range(2):
                sq = sum(dtile[i // 2, code[rr][i], h] for i in range(2 * stops))
                den[pl.ds(h, 1), pl.ds(rr * tile, tile)] = jnp.sum(sq, axis=0, keepdims=True)

    vturn[:, pl.ds(0, rows)] = kv0[1].reshape(rows, feat).T
    mask_keys(0)

    @pl.loop(0, cap // 4)
    def _(i):
        for k in range(4):
            eturn[4 * i + k] = (e0[4 * i + k].astype(jnp.float32) * scale).T

    for j in range(6):
        fc = place_at(j)
        remote(q_hbm, share(fc), q_send.at[j], q_recv.at[j], (b, pf)).wait_recv()
    weights(0)

    @pl.when(place == 1)
    def _():
        pass_on(1)

    def kv_wait(slot):
        for c in send_kv(0, slot, at(1)):
            c.wait_recv()

    def kv_forward(n, slot, to):
        return [
            remote(kvs[slot].at[i], kvs[to].at[i], kvf_send.at[n, i], kv_recv.at[to, i], at(1))
            for i in range(2)
        ]

    forwards = {
        1: {2: kv_forward(0, 1, 2)},
        2: {0: kv_forward(0, 2, 3), 2: kv_forward(1, 2, 3)},
        3: {0: kv_forward(1, 3, 2)},
    }
    for slots in ((1,), (2, 3)):
        for slot in slots:
            kv_wait(slot)
            for p, copies in forwards[slot].items():
                @pl.when(place == p)
                def _():
                    for c in copies:
                        c.start()
        weights(*slots)

    def n_copy(j):
        return [
            remote(sendbuf.at[j], nrecv.at[j], n_send.at[j], n_recv.at[j], (b, place_at(j))),
            remote(dsend.at[j], drecv.at[j], d_send.at[j], d_recv.at[j], (b, place_at(j))),
        ]

    @pl.loop(0, 7)
    def _(j):
        chunk(place_at(j), sendbuf.at[j], dsend.at[j])

        @pl.when(j > 0)
        def _():
            for c in n_copy(j - 1):
                c.start()

    chunk(f, numacc, dsend.at[7])
    for c in n_copy(6):
        c.start()

    den = dsend[7]
    for j in range(7):
        for c in n_copy(j):
            c.wait_recv()
        numacc[...] += nrecv[j].astype(jnp.float32)
        den = den + drecv[j]
    inverse = 1.0 / jnp.sqrt(1.0 + den)
    for h in range(HEADS):
        feats = pl.ds(h * dh, dh)
        sendbuf[7, feats] = (numacc[feats] * inverse[h:h + 1]).astype(jnp.bfloat16)
    out[...] = sendbuf[7].T

    for c in own_q + other_q + [inv_copy]:
        c.wait_send()
    for p in range(4):
        @pl.when(place == p)
        def _():
            for c in sends[p] + late[p]:
                c.wait_send()

    @pl.when(place == 1)
    def _():
        for i in range(2):
            relay_kv(i).wait_send()
            for ch in range(PARTS):
                relay_e(i, ch).wait_send()

    for slot in range(1, 4):
        for p, copies in forwards[slot].items():
            @pl.when(place == p)
            def _():
                for c in copies:
                    c.wait_send()
    for j in range(7):
        for c in n_copy(j):
            c.wait_send()


def on_device(queries, keys, values, tiles, edges):
    rows, feat = queries.shape
    stops, cap, tile = edges.shape[2], edges.shape[3], edges.shape[4]
    bf, f32, i32 = jnp.bfloat16, jnp.float32, jnp.int32
    dma = pltpu.SemaphoreType.DMA
    ebuf = pltpu.VMEM((cap, tile, tile), bf)
    kvbuf = pltpu.VMEM((2, rows // tile, tile, feat), bf)
    split = (rows // tile, tile, feat)
    lists = tiles.reshape(stops, cap)
    any_spec = pl.BlockSpec(memory_space=pl.ANY)
    return pl.pallas_call(
        kernel,
        out_shape=pltpu.VMEM((rows, feat), bf),
        in_specs=[pl.BlockSpec(memory_space=pltpu.SMEM), pl.BlockSpec(memory_space=pltpu.VMEM)] + [any_spec] * 4,
        out_specs=pl.BlockSpec(memory_space=pltpu.VMEM),
        scratch_shapes=[
            pltpu.VMEM((8 * rows // tile, tile, feat), bf),
            kvbuf, kvbuf, kvbuf, kvbuf,
            ebuf, ebuf, ebuf, ebuf, ebuf, ebuf,
            kvbuf,
            pltpu.VMEM((2, 16, 128), i32),
            pltpu.SMEM((2, 16, 128), i32),
            pltpu.VMEM((feat, stops * rows), bf),
            pltpu.VMEM((stops, 2, HEADS // 2, rows, feat // 2), bf),
            pltpu.VMEM((cap, tile, tile), f32),
            pltpu.VMEM((stops, cap + 1, HEADS, tile, tile), bf),
            pltpu.VMEM((stops, cap + 1, HEADS, 8, tile), f32),
            pltpu.VMEM((feat, rows), f32),
            pltpu.VMEM((8, feat, rows), bf),
            pltpu.VMEM((8, HEADS, rows), f32),
            pltpu.VMEM((7, feat, rows), bf),
            pltpu.VMEM((7, HEADS, rows), f32),
            dma((5,)), dma((7,)), dma((7,)), dma((4, PARTS)), dma((4, PARTS)),
            dma((2, 2)), dma((4, 2)), dma((2, 2)),
            dma((3, PARTS)), dma((3, PARTS)), dma((2,)),
            dma((7,)), dma((7,)), dma((7,)), dma((7,)),
        ],
        compiler_params=pltpu.CompilerParams(collective_id=0, has_side_effects=True),
    )(
        lists, lists, queries.reshape(split), keys.reshape(split), values.reshape(split),
        edges.reshape(stops, cap, tile, tile),
    )


def solution(mesh):
    return jax.shard_map(
        on_device,
        mesh=mesh,
        in_specs=(
            P(("blk", "fiber"), None),
            P(("blk", "fiber"), None),
            P(("blk", "fiber"), None),
            P("blk", "fiber", None, None),
            P("blk", "fiber", None, None, None, None),
        ),
        out_specs=P(("blk", "fiber"), None),
        check_vma=False,
    )
```
